32 devices in a mesh: replica: 8 (over z, core), shard: 4 (over y, x).
Axes of the slice: x: 2, y: 2, z: 4, core: 2. Of those that a mesh axis runs over, the one named last changes fastest.
Arguments:
- tokens: bfloat16 [32, 1024, 768], P(('replica', 'shard')), may hold values from -6 to 6
- segments: int32 [32, 1024], P(('replica', 'shard')), may hold values from 0 to 3, never falling along the last dimension, each value on 1 to 768 neighbouring positions
- attention_gain: bfloat16 [768], P('shard'), may hold values from 0.5 to 1.5
- attention_shift: bfloat16 [768], P('shard'), may hold values from -1.1953125 to 1.1953125
- input_weight: bfloat16 [768, 2304], P('shard'), may hold values from -0.21875 to 0.21875
- query_bias: bfloat16 [768], P('shard'), may hold values from -1.1953125 to 1.1953125
- value_bias: bfloat16 [768], P('shard'), may hold values from -1.1953125 to 1.1953125
- mixing_weight: bfloat16 [768, 768], P('shard'), may hold values from -0.875 to 0.875
- mixing_bias: bfloat16 [768], P('shard'), may hold values from -1.1953125 to 1.1953125
- dense_gain: bfloat16 [768], P('shard'), may hold values from 0.5 to 1.5
- dense_shift: bfloat16 [768], P('shard'), may hold values from -1.1953125 to 1.1953125
- expand_weight: bfloat16 [768, 3072], P('shard'), may hold values from -0.21875 to 0.21875
- expand_bias: bfloat16 [3072], P('shard'), may hold values from -1.1953125 to 1.1953125
- contract_weight: bfloat16 [3072, 768], P('shard'), may hold values from -0.109375 to 0.109375
- contract_bias: bfloat16 [768], P('shard'), may hold values from -1.1953125 to 1.1953125
- cotangent: bfloat16 [32, 1024, 768], P(('replica', 'shard')), may hold values from -6 to 6
Outputs:
- layer_output: bfloat16 [32, 1024, 768], P(('replica', 'shard'))
- tokens_gradient: bfloat16 [32, 1024, 768], P(('replica', 'shard'))
- attention_gain_gradient: float32 [768], P('shard')
- attention_shift_gradient: float32 [768], P('shard')
- input_weight_gradient: float32 [768, 2304], P('shard')
- query_bias_gradient: float32 [768], P('shard')
- value_bias_gradient: float32 [768], P('shard')
- mixing_weight_gradient: float32 [768, 768], P('shard')
- mixing_bias_gradient: float32 [768], P('shard')
- dense_gain_gradient: float32 [768], P('shard')
- dense_shift_gradient: float32 [768], P('shard')
- expand_weight_gradient: float32 [768, 3072], P('shard')
- expand_bias_gradient: float32 [3072], P('shard')
- contract_weight_gradient: float32 [3072, 768], P('shard')
- contract_bias_gradient: float32 [768], P('shard')
The draws below stay inside these ranges and needn't reach their ends.
Inputs may be any that keep to these rules, and one draw needn't show every extreme that they name: `segments`: within each sequence the document numbers start at 0 and rise by one from one document to the next; every document has 1 to 768 tokens and every token belongs to one.
All inputs are finite; a program needn't handle non-finite values.
Results may differ from the reference program's by a relative error of at most 0.019.
Values may be sent and summed in bfloat16 or wider, within the bound.
No kernel may reach another device: no remote copies, remote signals or barrier semaphores. Data moves between devices by JAX's collectives and lax.ppermute only.
A program may use at most 320 MiB of HBM per device.

```python
import math
import jax
import jax.numpy as jnp
import numpy as np
from jax import lax

D = 768
H = 12
HD = 64
FF = 3072
SEQ_LEN = 1024
NSEQ = 32


def block_levels(key, shape, split, low, high):
    factor_of = 1.0
    for position, parts in split:
        draws = jax.random.uniform(jax.random.fold_in(jax.random.fold_in(key, 6), position), (parts,), jnp.float32, low / len(split), high / len(split))
        factor_of = factor_of * jnp.repeat(jnp.exp(draws), shape[position] // parts).reshape((-1,) + (1,) * (len(shape) - 1 - position))
    return factor_of


def split_up(amount, total, bound, slope):
    portions = [(1 << 20) // math.isqrt(grade ** slope) + 1 for grade in range(2, amount + 1)]
    spare, given = total - bound - (amount - 1), [1] * (amount - 1)
    while spare > 0:
        free = [i for i in range(amount - 1) if given[i] < bound]
        mass, left = sum([portions[i] for i in free]), spare
        for i in free:
            extra = min(bound - given[i], max(1, left * portions[i] // mass), spare)
            given[i] = given[i] + extra
            spare = spare - extra
    return np.array([bound] + given)


def ragged(stream_key, count, total, reach, skew):
    if count == 2:
        one = jax.random.randint(stream_key, (), max(1, total - reach), min(reach, total - 1) + 1)
        return jnp.stack([one, total - one])
    lengths = jnp.asarray(split_up(count, total, reach, skew), jnp.int32)
    twos = (count - 1) // 2
    donor, receiver = lengths[1:1 + 2 * twos:2], lengths[2:2 + 2 * twos:2]
    room = jnp.minimum(donor - 1, reach - receiver)
    passed = jax.random.randint(jax.random.fold_in(stream_key, 1), (twos,), 0, 1 << 20) % (room + 1)
    lengths = lengths.at[1:1 + 2 * twos:2].set(donor - passed).at[2:2 + 2 * twos:2].set(receiver + passed)
    return lengths[jax.random.permutation(jax.random.fold_in(stream_key, 2), count)]


def normal_values(own_key, extent, deviation, reach, cuts=(), dtype=jnp.bfloat16):
    level = block_levels(own_key, extent, cuts, -0.22, 0.18) if cuts else 1.0
    drawn = jax.random.normal(own_key, extent, jnp.float32) * deviation * level
    return jnp.minimum(jnp.maximum(drawn, -reach), reach).astype(dtype)


def setup_inputs(seed: int = 0) -> dict:
    streams_of = jax.random.split(jax.random.key(seed), 17)
    return {
        "tokens": normal_values(streams_of[0], (NSEQ, SEQ_LEN, D), 1.0, 6.0, ((0, 32),)),
        "segments": jax.vmap(lambda own: jnp.searchsorted(jnp.cumsum(ragged(own, max(2, SEQ_LEN // 256), SEQ_LEN, SEQ_LEN * 3 // 4, 0)), jnp.arange(SEQ_LEN), side="right"))(jax.random.split(streams_of[1], NSEQ)).reshape((NSEQ, SEQ_LEN)).astype(jnp.int32),
        "attention_gain": jnp.clip(1.0 + 0.1 * jax.random.normal(streams_of[2], (D,), jnp.float32), 0.5, 1.5).astype(jnp.bfloat16),
        "attention_shift": normal_values(streams_of[3], (D,), 0.2, 1.1953125, ((0, 4),)),
        "input_weight": normal_values(streams_of[4], (D, 3 * D), D ** -0.5, 0.21875, ((0, 4),)),
        "query_bias": normal_values(streams_of[5], (D,), 0.2, 1.1953125, ((0, 4),)),
        "value_bias": normal_values(streams_of[6], (D,), 0.2, 1.1953125, ((0, 4),)),
        "mixing_weight": normal_values(streams_of[7], (D, D), (D // 16) ** -0.5, 0.875, ((0, 4),)),
        "mixing_bias": normal_values(streams_of[8], (D,), 0.2, 1.1953125, ((0, 4),)),
        "dense_gain": jnp.clip(1.0 + 0.1 * jax.random.normal(streams_of[9], (D,), jnp.float32), 0.5, 1.5).astype(jnp.bfloat16),
        "dense_shift": normal_values(streams_of[10], (D,), 0.2, 1.1953125, ((0, 4),)),
        "expand_weight": normal_values(streams_of[11], (D, FF), D ** -0.5, 0.21875, ((0, 4),)),
        "expand_bias": normal_values(streams_of[12], (FF,), 0.2, 1.1953125, ((0, 4),)),
        "contract_weight": normal_values(streams_of[13], (FF, D), FF ** -0.5, 0.109375, ((0, 4),)),
        "contract_bias": normal_values(streams_of[14], (D,), 0.2, 1.1953125, ((0, 4),)),
        "cotangent": normal_values(streams_of[15], (NSEQ, SEQ_LEN, D), 1.0, 6.0, ((0, 32),)),
    }


EPSILON = 1e-05
HIGHEST = lax.Precision.HIGHEST

@jax.custom_vjp
def low(v):
    return lax.optimization_barrier(v.astype(jnp.bfloat16)).astype(jnp.float32)

@jax.custom_vjp
def low_back(v):
    return v

def low_keep(v):
    return (low(v), None)

def low_pass(kept, grad):
    return (grad,)

def back_keep(v):
    return (v, None)

def back_low(kept, grad):
    return (low(grad),)
low.defvjp(low_keep, low_pass)
low_back.defvjp(back_keep, back_low)

def layer_norm(value, gain, shift):
    center = lax.optimization_barrier(jnp.mean(value, axis=-1, keepdims=True))
    centred = value - center
    spread = lax.optimization_barrier(jnp.mean(centred * centred, axis=-1, keepdims=True))
    return centred * lax.rsqrt(spread + EPSILON) * gain + shift

def block_forward(inputs, segment_rows, params):
    attention_gain, attention_shift, input_weight, query_bias, value_bias, mixing_weight, mixing_bias, dense_gain, dense_shift, expand_weight, expand_bias, contract_weight, contract_bias = params
    group_size, seq_rows, width = inputs.shape
    normed_one = low(layer_norm(inputs, attention_gain, attention_shift))
    bias_all = jnp.concatenate([query_bias, jnp.zeros_like(query_bias), value_bias])
    projected = jnp.einsum('gld,de->gle', normed_one, input_weight, precision=HIGHEST) + bias_all
    projected = low_back(low(projected))
    heads = projected.reshape(group_size, seq_rows, 3, H, HD)
    queries = heads[:, :, 0]
    key_rows = heads[:, :, 1]
    value_row_matrix = heads[:, :, 2]
    scores = jnp.einsum('glhd,gmhd->ghlm', queries, key_rows, precision=HIGHEST) * HD ** (-0.5)
    positions = jnp.arange(seq_rows)
    causal = positions[:, None] >= positions[None, :]
    allowed = (segment_rows[:, :, None] == segment_rows[:, None, :]) & causal[None]
    scores = low_back(jnp.where(allowed[:, None], scores, -1e+30))
    weight_matrices = low(jax.nn.softmax(scores, axis=-1))
    attended = jnp.einsum('ghlm,gmhd->glhd', weight_matrices, value_row_matrix, precision=HIGHEST)
    attended = low_back(low(attended.reshape(group_size, seq_rows, width)))
    branch_one = jnp.einsum('gld,de->gle', attended, mixing_weight, precision=HIGHEST) + mixing_bias
    middle = inputs + low_back(branch_one)
    normed_two = low(layer_norm(middle, dense_gain, dense_shift))
    hidden_pre = low_back(jnp.einsum('gld,df->glf', normed_two, expand_weight, precision=HIGHEST) + expand_bias)
    hidden_act = low(jax.nn.gelu(hidden_pre, approximate=True))
    branch_two = jnp.einsum('glf,fd->gld', hidden_act, contract_weight, precision=HIGHEST) + contract_bias
    return middle + low_back(branch_two)

def reference(tokens, segments, attention_gain, attention_shift, input_weight, query_bias, value_bias, mixing_weight, mixing_bias, dense_gain, dense_shift, expand_weight, expand_bias, contract_weight, contract_bias, cotangent):
    params = (attention_gain.astype(jnp.float32), attention_shift.astype(jnp.float32), input_weight.astype(jnp.float32), query_bias.astype(jnp.float32), value_bias.astype(jnp.float32), mixing_weight.astype(jnp.float32), mixing_bias.astype(jnp.float32), dense_gain.astype(jnp.float32), dense_shift.astype(jnp.float32), expand_weight.astype(jnp.float32), expand_bias.astype(jnp.float32), contract_weight.astype(jnp.float32), contract_bias.astype(jnp.float32))
    group_size = math.gcd(NSEQ, max(1, 4096 // SEQ_LEN))
    group_count = NSEQ // group_size
    token_groups = tokens.astype(jnp.float32).reshape(group_count, group_size, SEQ_LEN, D)
    segment_groups = segments.reshape(group_count, group_size, SEQ_LEN)
    stepper = jax.checkpoint(block_forward)

    def forward(inputs, weight_matrices):

        def one_group(packed):
            return stepper(packed[0], packed[1], weight_matrices)
        return lax.map(one_group, (inputs, segment_groups))
    result, pullback = jax.vjp(forward, token_groups, params)
    grad_tokens, grad_params = pullback(cotangent.astype(jnp.float32).reshape(group_count, group_size, SEQ_LEN, D))
    gain_one, shift_one, input_grad, query_grad, value_grad, mixing_grad, mixer_bias_gradient, gain_two, shift_two, expand_grad, expand_bias_grad, contract_grad, contract_bias_grad = grad_params
    return (result.reshape(NSEQ, SEQ_LEN, D).astype(jnp.bfloat16), grad_tokens.reshape(NSEQ, SEQ_LEN, D).astype(jnp.bfloat16), gain_one, shift_one, input_grad, query_grad, value_grad, mixing_grad, mixer_bias_gradient, gain_two, shift_two, expand_grad, expand_bias_grad, contract_grad, contract_bias_grad)
```

```python
import functools

import jax
import jax.numpy as jnp
from jax import lax
from jax.experimental import pallas as pl
from jax.experimental.pallas import tpu as pltpu
from jax.sharding import PartitionSpec as P

H = 12
HD = 64
LANES = 128
EPSILON = 1e-05
NEG = -1e30
VMEM_LIMIT = 56 * 1024 * 1024


F32 = jnp.float32
BF16 = jnp.bfloat16


def layer_norm(value, gain, shift):
    center = jnp.mean(value, axis=-1, keepdims=True)
    centred = value - center
    spread = jnp.mean(centred * centred, axis=-1, keepdims=True)
    return centred * lax.rsqrt(spread + EPSILON) * gain + shift


def gelu_tanh(value):
    return jax.nn.gelu(value, approximate=True)


def matmul(left, right):
    return jnp.dot(left, right, preferred_element_type=F32)


def dot_cols(left, right):
    return lax.dot_general(left, right, (((1,), (1,)), ((), ())), preferred_element_type=F32)


def dot_rows(left, right):
    return lax.dot_general(left, right, (((0,), (0,)), ((), ())), preferred_element_type=F32)


def swap(value, axis, bit):
    count = lax.axis_size(axis)
    return lax.ppermute(value, axis, [(i, i ^ bit) for i in range(count)])


def attend_forward_kernel(q_ref, k_ref, v_ref, segc_ref, segr_ref, o_ref, lse_ref, bias_ref, *, block):
    rows = q_ref.shape[0]

    @pl.when(pl.program_id(0) == 0)
    def _():
        for first in range(0, rows, block):
            keys = first + block
            row_id = first + lax.broadcasted_iota(jnp.int32, (block, keys), 0)
            key_id = lax.broadcasted_iota(jnp.int32, (block, keys), 1)
            allowed = (segc_ref[first:keys, :] == segr_ref[:, :keys]) & (row_id >= key_id)
            bias_ref[first:keys, :keys] = jnp.where(allowed, 0.0, NEG)

    lane = lax.broadcasted_iota(jnp.int32, (1, LANES), 1)
    scale = jnp.asarray(HD ** (-0.5), BF16)
    for first in range(0, rows, block):
        keys = first + block
        query = q_ref[first:keys, :] * scale
        key_rows = k_ref[:keys, :]
        value_rows = v_ref[:keys, :]
        parts = []
        for head in range(LANES // HD):
            mine = lane // HD == head
            one = jnp.where(mine, query, jnp.zeros_like(query))
            score = dot_cols(one, key_rows) + bias_ref[first:keys, :keys]
            peak = jnp.max(score, axis=1, keepdims=True)
            expo = jnp.exp(score - peak)
            total = jnp.sum(expo, axis=1, keepdims=True)
            out = matmul(expo.astype(BF16), value_rows) / total
            parts.append(jnp.where(mine, out, 0.0))
            log_total = jnp.broadcast_to(peak + jnp.log(total), (block, LANES))
            lse_ref[0, head : head + 1, first:keys] = log_total.T[0:1, :]
        o_ref[first:keys, :] = sum(parts).astype(BF16)


def attend_forward(projected, segment_row):
    rows = projected.shape[0]
    width = projected.shape[1] // 3
    pairs = width // LANES
    block = min(256, rows)
    column = lambda part: pl.BlockSpec((rows, LANES), lambda i: (0, part * pairs + i))
    return pl.pallas_call(
        functools.partial(attend_forward_kernel, block=block),
        grid=(pairs,),
        in_specs=[
            column(0),
            column(1),
            column(2),
            pl.BlockSpec((rows, 1), lambda i: (0, 0)),
            pl.BlockSpec((1, rows), lambda i: (0, 0)),
        ],
        out_specs=[
            pl.BlockSpec((rows, LANES), lambda i: (0, i)),
            pl.BlockSpec((1, 8, rows), lambda i: (i, 0, 0)),
        ],
        out_shape=[
            jax.ShapeDtypeStruct((rows, width), BF16),
            jax.ShapeDtypeStruct((pairs, 8, rows), F32),
        ],
        scratch_shapes=[pltpu.VMEM((rows, rows), F32)],
        compiler_params=pltpu.CompilerParams(vmem_limit_bytes=VMEM_LIMIT),
        name="attend_forward",
    )(projected, projected, projected, segment_row.reshape(rows, 1), segment_row.reshape(1, rows))


def attend_backward_kernel(
    q_ref, k_ref, v_ref, segc_ref, segr_ref, lse_ref, do_ref, out_ref, bias_ref, dk_ref, dv_ref, stage_ref, sem, *, block
):
    rows = q_ref.shape[0]
    step = pl.program_id(0)
    steps = pl.num_programs(0)

    @pl.when(step == 0)
    def _():
        for first in range(0, rows, block):
            keys = first + block
            key_id = lax.broadcasted_iota(jnp.int32, (keys, block), 0)
            row_id = first + lax.broadcasted_iota(jnp.int32, (keys, block), 1)
            allowed = (segc_ref[:keys, :] == segr_ref[:, first:keys]) & (row_id >= key_id)
            bias_ref[:keys, first:keys] = jnp.where(allowed, 0.0, NEG)

    slot = step % 2

    def copies(at_step, at_slot):
        return [
            pltpu.make_async_copy(
                stage_ref.at[at_slot, part],
                out_ref.at[:, pl.ds(pl.multiple_of((part * steps + at_step) * LANES, LANES), LANES)],
                sem.at[at_slot, part],
            )
            for part in range(3)
        ]

    @pl.when(step >= 2)
    def _():
        for copy in copies(step - 2, slot):
            copy.wait()

    lane = lax.broadcasted_iota(jnp.int32, (1, LANES), 1)
    scale = jnp.asarray(HD ** (-0.5), BF16)
    for first in range(0, rows, block):
        keys = first + block
        query = q_ref[first:keys, :] * scale
        grad = do_ref[first:keys, :]
        key_rows = k_ref[:keys, :]
        value_rows = v_ref[:keys, :]
        shares, slopes, queries, grads, parts = [], [], [], [], []
        for head in range(LANES // HD):
            mine = lane // HD == head
            one = jnp.where(mine, query, jnp.zeros_like(query))
            one_grad = jnp.where(mine, grad, jnp.zeros_like(grad))
            score = dot_cols(key_rows, one) + bias_ref[:keys, first:keys]
            share = jnp.exp(score - lse_ref[0, head : head + 1, first:keys])
            grad_share = dot_cols(value_rows, one_grad)
            center = jnp.sum(share * grad_share, axis=0, keepdims=True)
            slope = (share * (grad_share - center)).astype(BF16)
            shares.append(share.astype(BF16))
            slopes.append(slope)
            queries.append(one)
            grads.append(one_grad)
            parts.append(jnp.where(mine, dot_rows(slope, key_rows), 0.0))
        value_part = sum(matmul(a, b) for a, b in zip(shares, grads))
        key_part = sum(matmul(a, b) for a, b in zip(slopes, queries))
        if first > 0:
            dv_ref[:first, :] += value_part[:first]
            dk_ref[:first, :] += key_part[:first]
        dv_ref[first:keys, :] = value_part[first:]
        dk_ref[first:keys, :] = key_part[first:]
        stage_ref[slot, 0, first:keys, :] = (sum(parts) * (HD ** (-0.5))).astype(BF16)
    stage_ref[slot, 1] = dk_ref[...].astype(BF16)
    stage_ref[slot, 2] = dv_ref[...].astype(BF16)
    for copy in copies(step, slot):
        copy.start()

    @pl.when(step == steps - 1)
    def _():
        if out_ref.shape[1] // (3 * LANES) > 1:
            for copy in copies(step - 1, 1 - slot):
                copy.wait()
        for copy in copies(step, slot):
            copy.wait()


def attend_backward(projected, segment_row, log_totals, grad_out):
    rows = projected.shape[0]
    width = projected.shape[1] // 3
    pairs = width // LANES
    block = min(256, rows)
    column = lambda part: pl.BlockSpec((rows, LANES), lambda i: (0, part * pairs + i))
    return pl.pallas_call(
        functools.partial(attend_backward_kernel, block=block),
        grid=(pairs,),
        in_specs=[
            column(0),
            column(1),
            column(2),
            pl.BlockSpec((rows, 1), lambda i: (0, 0)),
            pl.BlockSpec((1, rows), lambda i: (0, 0)),
            pl.BlockSpec((1, 8, rows), lambda i: (i, 0, 0)),
            pl.BlockSpec((rows, LANES), lambda i: (0, i)),
        ],
        out_specs=pl.BlockSpec(memory_space=pl.ANY),
        out_shape=jax.ShapeDtypeStruct((rows, 3 * width), BF16),
        scratch_shapes=[
            pltpu.VMEM((rows, rows), F32),
            pltpu.VMEM((rows, LANES), F32),
            pltpu.VMEM((rows, LANES), F32),
            pltpu.VMEM((2, 3, rows, LANES), BF16),
            pltpu.SemaphoreType.DMA((2, 3)),
        ],
        compiler_params=pltpu.CompilerParams(vmem_limit_bytes=VMEM_LIMIT),
        name="attend_backward",
    )(
        projected,
        projected,
        projected,
        segment_row.reshape(rows, 1),
        segment_row.reshape(1, rows),
        log_totals,
        grad_out,
    )


def assemble_kernel(place_ref, own_ref, *refs, keys, rows, half):
    count = len(keys)
    parts, out_ref, sem = refs[: 2 * count], refs[2 * count], refs[2 * count + 1]
    core = place_ref[0]
    mine = place_ref[1]
    copies = [
        pltpu.make_async_copy(
            own_ref, out_ref.at[pl.ds(pl.multiple_of(mine * rows, 16), rows), :], sem.at[2 * count]
        )
    ]
    for index, (other, first, size) in enumerate(keys):
        for side in range(2):
            ref = parts[side * count + index]
            row = pl.multiple_of((mine ^ other) * rows + first, 16)
            col = pl.multiple_of((core ^ side) * half, LANES)
            copies.append(
                pltpu.make_async_copy(
                    ref, out_ref.at[pl.ds(row, size), pl.ds(col, half)], sem.at[side * count + index]
                )
            )
    for copy in copies:
        copy.start()
    for copy in copies:
        copy.wait()


def bit_list(count):
    bits, bit = [], 1
    while bit < count:
        bits.append(bit)
        bit *= 2
    return bits


def gather_weight(weight, place, split):
    rows, cols = weight.shape
    half = cols // 2
    shards_count = lax.axis_size("shard")
    mine = lax.dynamic_slice(weight, (0, place[0] * half), (rows, half))
    bits = bit_list(shards_count)
    size = rows // split
    keys, near = [], []
    for piece in range(split):
        order = bits if piece % 2 == 0 else bits[::-1]
        if split == 1:
            blocks = {0: mine}
        else:
            blocks = {0: mine[piece * size : (piece + 1) * size]}
        for bit in order:
            blocks.update({j ^ bit: swap(blocks[j], "shard", bit) for j in list(blocks)})
        for j in sorted(blocks):
            if j:
                keys.append((j, piece * size, size))
                near.append(blocks[j])
    far = [swap(block, "replica", 1) for block in near]
    count = len(keys)
    return pl.pallas_call(
        functools.partial(assemble_kernel, keys=tuple(keys), rows=rows, half=half),
        grid_spec=pltpu.PrefetchScalarGridSpec(
            num_scalar_prefetch=1,
            in_specs=[pl.BlockSpec(memory_space=pl.ANY)] * (2 * count + 1),
            out_specs=pl.BlockSpec(memory_space=pl.ANY),
            scratch_shapes=[pltpu.SemaphoreType.DMA((2 * count + 1,))],
        ),
        out_shape=jax.ShapeDtypeStruct((rows * shards_count, cols), weight.dtype),
        name="assemble",
    )(place, weight, *near, *far)


def gather_small(vectors, place):
    sizes = [v.shape[0] for v in vectors]
    packed = jnp.concatenate(vectors)
    packed = packed.reshape(1, packed.shape[0])
    shards_count = lax.axis_size("shard")
    blocks = [packed if j == 0 else swap(packed, "shard", j) for j in range(shards_count)]
    for bit in bit_list(shards_count):
        here = (place[1] & bit) != 0
        blocks = [jnp.where(here, blocks[j ^ bit], blocks[j]) for j in range(shards_count)]
    whole = jnp.concatenate(blocks, axis=0).astype(F32)
    out, first = [], 0
    for size in sizes:
        out.append(whole[:, first : first + size].reshape(shards_count * size))
        first += size
    return out


def halvings(rows, replicas):
    parts = 1
    while 2 * parts < replicas and rows % (32 * parts) == 0:
        parts *= 2
    return parts


def weight_gradient_kernel(place_ref, lhs_ref, rhs_ref, *refs, order, parts, size, add, steps):
    if add:
        recv_ref, keep_ref, send_ref, turned_ref, sorted_ref = refs
    else:
        send_ref, turned_ref, sorted_ref = refs
    mine, level = place_ref[1], place_ref[2]
    rows = parts * size

    @pl.when(pl.program_id(1) == 0)
    def _():
        turned_ref[...] = lhs_ref[...].T
        for index, other in enumerate(order if steps == 1 else (0,)):
            for part in range(parts):
                shard = (mine ^ other) if steps == 1 else 0
                first = pl.multiple_of(shard * rows + (level ^ part) * size, 16)
                sorted_ref[index * rows + part * size : index * rows + (part + 1) * size, :] = turned_ref[
                    pl.ds(first, size), :
                ]

    total = matmul(sorted_ref[...], rhs_ref[...])
    if not add:
        send_ref[...] = total.astype(BF16)
        return
    total = (total + recv_ref[...].astype(F32)).astype(BF16)
    if steps == 1:
        middle = total.shape[0] // 2
        keep_ref[...] = total[:middle]
        send_ref[...] = total[middle:]
    else:
        step = pl.program_id(0)

        @pl.when(step < steps // 2)
        def _():
            keep_ref[...] = total

        @pl.when(step >= steps // 2)
        def _():
            send_ref[...] = total


def weight_gradient(left, right, place, order, steps, chunk, received=None):
    tokens, rows_all = left.shape
    half = right.shape[1] // 2
    shards_count = len(order)
    rows = rows_all // shards_count
    parts = halvings(rows, lax.axis_size("replica"))
    size = rows // parts
    add = received is not None
    block = rows_all // steps
    chunks = half // chunk
    side = 0 if add else 1
    if steps == 1:
        left_spec = pl.BlockSpec((tokens, rows_all), lambda i, j, p: (0, 0))
    else:
        left_spec = pl.BlockSpec((tokens, block), lambda i, j, p: (0, p[1] ^ i))
    in_specs = [
        left_spec,
        pl.BlockSpec((tokens, chunk), lambda i, j, p: (0, (p[0] ^ side) * chunks + j)),
    ]
    whole = pl.BlockSpec((block, chunk), lambda i, j, p: (i, j))
    shape = lambda count: jax.ShapeDtypeStruct((count, half), BF16)
    if add:
        in_specs.append(whole)
        if steps == 1:
            part_spec = pl.BlockSpec((block // 2, chunk), lambda i, j, p: (0, j))
            out_specs = [part_spec, part_spec]
        else:
            middle = steps // 2
            out_specs = [
                pl.BlockSpec((block, chunk), lambda i, j, p: (jnp.minimum(i, middle - 1), j)),
                pl.BlockSpec((block, chunk), lambda i, j, p: (jnp.maximum(i - middle, 0), j)),
            ]
        out_shape = [shape(rows_all // 2), shape(rows_all // 2)]
    else:
        out_specs = whole
        out_shape = shape(rows_all)
    args = (left, right) + ((received,) if add else ())
    return pl.pallas_call(
        functools.partial(
            weight_gradient_kernel, order=tuple(order), parts=parts, size=size, add=add, steps=steps
        ),
        grid_spec=pltpu.PrefetchScalarGridSpec(
            num_scalar_prefetch=1,
            grid=(steps, chunks),
            in_specs=in_specs,
            out_specs=out_specs,
            scratch_shapes=[pltpu.VMEM((block, tokens), BF16), pltpu.VMEM((block, tokens), BF16)],
        ),
        out_shape=out_shape,
        compiler_params=pltpu.CompilerParams(vmem_limit_bytes=VMEM_LIMIT),
        name="weight_gradient",
    )(place, *args)


def add_low(left, right):
    return (left.astype(F32) + right.astype(F32)).astype(BF16)


def finish_kernel(place_ref, near_ref, far_ref, out_ref):
    out_ref[...] = jnp.where(pl.program_id(0) == 0, near_ref[...], far_ref[...]).astype(F32)


def reduce_rest(keep, send, place, bits, rows):
    half = keep.shape[1]
    replicas = lax.axis_size("replica")
    parts = halvings(rows, replicas)
    size = rows // parts
    for index, bit in enumerate(bits):
        total = add_low(keep, swap(send, "shard", bit))
        if index + 1 < len(bits):
            middle = total.shape[0] // 2
            keep, send = total[:middle], total[middle:]
    levels = bit_list(replicas)[1:]
    for bit in levels:
        if bit < 2 * parts:
            grid = total.reshape(total.shape[0] // (2 * size), 2, size, half)
            keep, send = grid[:, 0].reshape(-1, half), grid[:, 1].reshape(-1, half)
            total = add_low(keep, swap(send, "replica", bit))
        else:
            total = add_low(total, swap(total, "replica", bit))
    blocks = {0: total}
    for bit in reversed([b for b in levels if b < 2 * parts]):
        there = {j ^ (bit // 2): swap(blocks[j], "replica", bit) for j in list(blocks)}
        blocks.update(there)
    near = jnp.concatenate([blocks[j] for j in range(parts)], axis=0) if parts > 1 else total
    far = swap(near, "replica", 1)
    return pl.pallas_call(
        finish_kernel,
        grid_spec=pltpu.PrefetchScalarGridSpec(
            num_scalar_prefetch=1,
            grid=(2, parts),
            in_specs=[
                pl.BlockSpec((size, half), lambda i, j, p: (j, 0)),
                pl.BlockSpec((size, half), lambda i, j, p: (j, 0)),
            ],
            out_specs=pl.BlockSpec((size, half), lambda i, j, p: (p[2] % parts ^ j, p[0] ^ i)),
        ),
        out_shape=jax.ShapeDtypeStruct((rows, 2 * half), F32),
        name="finish",
    )(place, near, far)


def exchange_order(bits):
    order = [0]
    for bit in reversed(bits):
        order = order + [j ^ bit for j in order]
    return order


def reduce_small(parts, place):
    shards_count = lax.axis_size("shard")
    packed = jnp.concatenate([v.reshape(shards_count, -1) for v in parts], axis=1)
    for bit in bit_list(lax.axis_size("replica")):
        packed = packed + swap(packed, "replica", bit)
    for bit in bit_list(shards_count):
        packed = packed + swap(packed, "shard", bit)
    row = lax.dynamic_slice(packed, (place[1], 0), (1, packed.shape[1]))[0]
    out, first = [], 0
    for v in parts:
        size = v.shape[0] // shards_count
        out.append(row[first : first + size])
        first += size
    return out


def shards(
    tokens,
    segments,
    attention_gain,
    attention_shift,
    input_weight,
    query_bias,
    value_bias,
    mixing_weight,
    mixing_bias,
    dense_gain,
    dense_shift,
    expand_weight,
    expand_bias,
    contract_weight,
    contract_bias,
    cotangent,
):
    replica = lax.axis_index("replica")
    shard = lax.axis_index("shard")
    place = jnp.stack([replica & 1, shard, replica >> 1]).astype(jnp.int32)
    shards_count = lax.axis_size("shard")
    (
        gain_one,
        shift_one,
        query_full,
        value_full,
        mixing_bias_full,
        gain_two,
        shift_two,
        expand_bias_full,
        contract_bias_full,
    ) = gather_small(
        [
            attention_gain,
            attention_shift,
            query_bias,
            value_bias,
            mixing_bias,
            dense_gain,
            dense_shift,
            expand_bias,
            contract_bias,
        ],
        place,
    )
    input_full = gather_weight(input_weight, place, 2)
    mixing_full = gather_weight(mixing_weight, place, 1)
    expand_full = gather_weight(expand_weight, place, 2)
    contract_full = gather_weight(contract_weight, place, 2)
    seq_count, seq_rows, width = tokens.shape
    row_count = seq_count * seq_rows
    inputs = tokens.astype(F32).reshape(row_count, width)
    normed_one, norm_one_back = jax.vjp(layer_norm, inputs, gain_one, shift_one)
    normed_low = normed_one.astype(BF16)
    bias_all = jnp.concatenate([query_full, jnp.zeros_like(query_full), value_full])
    projected = (matmul(normed_low, input_full) + bias_all).astype(BF16)

    def rows_of(array, index):
        return array if seq_count == 1 else array[index * seq_rows : (index + 1) * seq_rows]

    def join(arrays):
        return arrays[0] if seq_count == 1 else jnp.concatenate(arrays, axis=0)

    forwards = [
        attend_forward(rows_of(projected, index), segments[index]) for index in range(seq_count)
    ]
    mixed_in = join([pair[0] for pair in forwards])
    middle = inputs + matmul(mixed_in, mixing_full) + mixing_bias_full
    normed_two, norm_two_back = jax.vjp(layer_norm, middle, gain_two, shift_two)
    normed_two_low = normed_two.astype(BF16)
    hidden_pre = matmul(normed_two_low, expand_full) + expand_bias_full
    hidden_full, gelu_back = jax.vjp(gelu_tanh, hidden_pre)
    hidden_act = hidden_full.astype(BF16)
    result = middle + matmul(hidden_act, contract_full) + contract_bias_full
    layer_output = result.astype(BF16).reshape(seq_count, seq_rows, width)

    bits = bit_list(shards_count)
    forth, back = bits, bits[::-1]
    order_forth, order_back = exchange_order(forth), exchange_order(back)
    identity = order_back == list(range(shards_count))
    grad_branch = cotangent.reshape(row_count, width)
    grad_result = grad_branch.astype(F32)
    contract_steps = shards_count if identity else 1
    contract_chunk = width // 2
    contract_sent = weight_gradient(
        hidden_act, grad_branch, place, order_back, contract_steps, contract_chunk
    )
    contract_got = swap(contract_sent, "replica", 1)
    grad_hidden = dot_cols(grad_branch, contract_full)
    grad_pre = gelu_back(grad_hidden)[0].astype(BF16)
    contract_pair = weight_gradient(
        hidden_act, grad_branch, place, order_back, contract_steps, contract_chunk, contract_got
    )
    contract_total = reduce_rest(*contract_pair, place, back, contract_weight.shape[0])
    expand_sent = weight_gradient(normed_two_low, grad_pre, place, order_forth, 1, 512)
    expand_got = swap(expand_sent, "replica", 1)
    grad_normed_two = dot_cols(grad_pre, expand_full)
    expand_pair = weight_gradient(
        normed_two_low, grad_pre, place, order_forth, 1, 512, expand_got
    )
    expand_total = reduce_rest(*expand_pair, place, forth, expand_weight.shape[0])
    contract_bias_grad = jnp.sum(grad_result, axis=0)
    expand_bias_grad = jnp.sum(grad_pre, axis=0, dtype=F32)
    grad_middle_norm, gain_two_grad, shift_two_grad = norm_two_back(grad_normed_two)
    grad_middle = grad_result + grad_middle_norm
    grad_mix = grad_middle.astype(BF16)
    mixing_bias_grad = jnp.sum(grad_mix, axis=0, dtype=F32)
    grad_attended = dot_cols(grad_mix, mixing_full).astype(BF16)
    mixing_sent = weight_gradient(mixed_in, grad_mix, place, order_back, 1, width // 2)
    mixing_got = swap(mixing_sent, "replica", 1)
    grad_projected = join(
        [
            attend_backward(
                rows_of(projected, index),
                segments[index],
                forwards[index][1],
                rows_of(grad_attended, index),
            )
            for index in range(seq_count)
        ]
    )
    mixing_pair = weight_gradient(
        mixed_in, grad_mix, place, order_back, 1, width // 2, mixing_got
    )
    mixing_total = reduce_rest(*mixing_pair, place, back, mixing_weight.shape[0])
    input_sent = weight_gradient(normed_low, grad_projected, place, order_forth, 1, width // 2)
    input_got = swap(input_sent, "replica", 1)
    projected_bias_grad = jnp.sum(grad_projected, axis=0, dtype=F32)
    query_grad = projected_bias_grad[:width]
    value_grad = projected_bias_grad[2 * width :]
    input_pair = weight_gradient(
        normed_low, grad_projected, place, order_forth, 1, width // 2, input_got
    )
    input_total = reduce_rest(*input_pair, place, forth, input_weight.shape[0])
    grad_normed_one = dot_cols(grad_projected, input_full)
    grad_inputs_norm, gain_one_grad, shift_one_grad = norm_one_back(grad_normed_one)
    tokens_gradient = (grad_middle + grad_inputs_norm).astype(BF16).reshape(seq_count, seq_rows, width)
    (
        attention_gain_total,
        attention_shift_total,
        query_total,
        value_total,
        mixing_bias_total,
        dense_gain_total,
        dense_shift_total,
        expand_bias_total,
        contract_bias_total,
    ) = reduce_small(
        [
            gain_one_grad,
            shift_one_grad,
            query_grad,
            value_grad,
            mixing_bias_grad,
            gain_two_grad,
            shift_two_grad,
            expand_bias_grad,
            contract_bias_grad,
        ],
        place,
    )
    return (
        layer_output,
        tokens_gradient,
        attention_gain_total,
        attention_shift_total,
        input_total,
        query_total,
        value_total,
        mixing_total,
        mixing_bias_total,
        dense_gain_total,
        dense_shift_total,
        expand_total,
        expand_bias_total,
        contract_total,
        contract_bias_total,
    )


def solution(mesh):
    return jax.shard_map(
        shards,
        mesh=mesh,
        in_specs=(
            P(("replica", "shard"), None, None),
            P(("replica", "shard"), None),
            P("shard"),
            P("shard"),
            P("shard", None),
            P("shard"),
            P("shard"),
            P("shard", None),
            P("shard"),
            P("shard"),
            P("shard"),
            P("shard", None),
            P("shard"),
            P("shard", None),
            P("shard"),
            P(("replica", "shard"), None, None),
        ),
        out_specs=(
            P(("replica", "shard"), None, None),
            P(("replica", "shard"), None, None),
            P("shard"),
            P("shard"),
            P("shard", None),
            P("shard"),
            P("shard"),
            P("shard", None),
            P("shard"),
            P("shard"),
            P("shard"),
            P("shard", None),
            P("shard"),
            P("shard", None),
            P("shard"),
        ),
        check_vma=False,
    )
```

```python
import functools

import jax
import jax.numpy as jnp
from jax import lax
from jax.experimental import pallas as pl
from jax.experimental.pallas import tpu as pltpu
from jax.sharding import PartitionSpec as P

H = 12
HD = 64
LANES = 128
EPSILON = 1e-05
NEG = -1e30
VMEM_LIMIT = 56 * 1024 * 1024


F32 = jnp.float32
BF16 = jnp.bfloat16


def layer_norm(value, gain, shift):
    center = jnp.mean(value, axis=-1, keepdims=True)
    centred = value - center
    spread = jnp.mean(centred * centred, axis=-1, keepdims=True)
    return centred * lax.rsqrt(spread + EPSILON) * gain + shift


def gelu_tanh(value):
    return jax.nn.gelu(value, approximate=True)


def matmul(left, right):
    return jnp.dot(left, right, preferred_element_type=F32)


def dot_cols(left, right):
    return lax.dot_general(left, right, (((1,), (1,)), ((), ())), preferred_element_type=F32)


def dot_rows(left, right):
    return lax.dot_general(left, right, (((0,), (0,)), ((), ())), preferred_element_type=F32)


def swap(value, axis, bit):
    count = lax.axis_size(axis)
    return lax.ppermute(value, axis, [(i, i ^ bit) for i in range(count)])


def attend_forward_kernel(q_ref, k_ref, v_ref, segc_ref, segr_ref, o_ref, lse_ref, bias_ref, *, block):
    rows = q_ref.shape[0]

    @pl.when(pl.program_id(0) == 0)
    def _():
        for first in range(0, rows, block):
            keys = first + block
            row_id = first + lax.broadcasted_iota(jnp.int32, (block, keys), 0)
            key_id = lax.broadcasted_iota(jnp.int32, (block, keys), 1)
            allowed = (segc_ref[first:keys, :] == segr_ref[:, :keys]) & (row_id >= key_id)
            bias_ref[first:keys, :keys] = jnp.where(allowed, 0.0, NEG)

    lane = lax.broadcasted_iota(jnp.int32, (1, LANES), 1)
    scale = jnp.asarray(HD ** (-0.5), BF16)
    for first in range(0, rows, block):
        keys = first + block
        query = q_ref[first:keys, :] * scale
        key_rows = k_ref[:keys, :]
        value_rows = v_ref[:keys, :]
        parts = []
        for head in range(LANES // HD):
            mine = lane // HD == head
            one = jnp.where(mine, query, jnp.zeros_like(query))
            score = dot_cols(one, key_rows) + bias_ref[first:keys, :keys]
            peak = jnp.max(score, axis=1, keepdims=True)
            expo = jnp.exp(score - peak)
            total = jnp.sum(expo, axis=1, keepdims=True)
            out = matmul(expo.astype(BF16), value_rows) / total
            parts.append(jnp.where(mine, out, 0.0))
            log_total = jnp.broadcast_to(peak + jnp.log(total), (block, LANES))
            lse_ref[0, head : head + 1, first:keys] = log_total.T[0:1, :]
        o_ref[first:keys, :] = sum(parts).astype(BF16)


def attend_forward(projected, segment_row):
    rows = projected.shape[0]
    width = projected.shape[1] // 3
    pairs = width // LANES
    block = min(256, rows)
    column = lambda part: pl.BlockSpec((rows, LANES), lambda i: (0, part * pairs + i))
    return pl.pallas_call(
        functools.partial(attend_forward_kernel, block=block),
        grid=(pairs,),
        in_specs=[
            column(0),
            column(1),
            column(2),
            pl.BlockSpec((rows, 1), lambda i: (0, 0)),
            pl.BlockSpec((1, rows), lambda i: (0, 0)),
        ],
        out_specs=[
            pl.BlockSpec((rows, LANES), lambda i: (0, i)),
            pl.BlockSpec((1, 8, rows), lambda i: (i, 0, 0)),
        ],
        out_shape=[
            jax.ShapeDtypeStruct((rows, width), BF16),
            jax.ShapeDtypeStruct((pairs, 8, rows), F32),
        ],
        scratch_shapes=[pltpu.VMEM((rows, rows), F32)],
        compiler_params=pltpu.CompilerParams(vmem_limit_bytes=VMEM_LIMIT),
        name="attend_forward",
    )(projected, projected, projected, segment_row.reshape(rows, 1), segment_row.reshape(1, rows))


def attend_backward_kernel(
    q_ref, k_ref, v_ref, segc_ref, segr_ref, lse_ref, do_ref, out_ref, bias_ref, dk_ref, dv_ref, stage_ref, sem, *, block
):
    rows = q_ref.shape[0]
    step = pl.program_id(0)
    steps = pl.num_programs(0)

    @pl.when(step == 0)
    def _():
        for first in range(0, rows, block):
            keys = first + block
            key_id = lax.broadcasted_iota(jnp.int32, (keys, block), 0)
            row_id = first + lax.broadcasted_iota(jnp.int32, (keys, block), 1)
            allowed = (segc_ref[:keys, :] == segr_ref[:, first:keys]) & (row_id >= key_id)
            bias_ref[:keys, first:keys] = jnp.where(allowed, 0.0, NEG)

    slot = step % 2

    def copies(at_step, at_slot):
        return [
            pltpu.make_async_copy(
                stage_ref.at[at_slot, part],
                out_ref.at[:, pl.ds(pl.multiple_of((part * steps + at_step) * LANES, LANES), LANES)],
                sem.at[at_slot, part],
            )
            for part in range(3)
        ]

    @pl.when(step >= 2)
    def _():
        for copy in copies(step - 2, slot):
            copy.wait()

    lane = lax.broadcasted_iota(jnp.int32, (1, LANES), 1)
    scale = jnp.asarray(HD ** (-0.5), BF16)
    for first in range(0, rows, block):
        keys = first + block
        query = q_ref[first:keys, :] * scale
        grad = do_ref[first:keys, :]
        key_rows = k_ref[:keys, :]
        value_rows = v_ref[:keys, :]
        shares, slopes, queries, grads, parts = [], [], [], [], []
        for head in range(LANES // HD):
            mine = lane // HD == head
            one = jnp.where(mine, query, jnp.zeros_like(query))
            one_grad = jnp.where(mine, grad, jnp.zeros_like(grad))
            score = dot_cols(key_rows, one) + bias_ref[:keys, first:keys]
            share = jnp.exp(score - lse_ref[0, head : head + 1, first:keys])
            grad_share = dot_cols(value_rows, one_grad)
            center = jnp.sum(share * grad_share, axis=0, keepdims=True)
            slope = (share * (grad_share - center)).astype(BF16)
            shares.append(share.astype(BF16))
            slopes.append(slope)
            queries.append(one)
            grads.append(one_grad)
            parts.append(jnp.where(mine, dot_rows(slope, key_rows), 0.0))
        value_part = sum(matmul(a, b) for a, b in zip(shares, grads))
        key_part = sum(matmul(a, b) for a, b in zip(slopes, queries))
        if first > 0:
            dv_ref[:first, :] += value_part[:first]
            dk_ref[:first, :] += key_part[:first]
        dv_ref[first:keys, :] = value_part[first:]
        dk_ref[first:keys, :] = key_part[first:]
        stage_ref[slot, 0, first:keys, :] = (sum(parts) * (HD ** (-0.5))).astype(BF16)
    stage_ref[slot, 1] = dk_ref[...].astype(BF16)
    stage_ref[slot, 2] = dv_ref[...].astype(BF16)
    for copy in copies(step, slot):
        copy.start()

    @pl.when(step == steps - 1)
    def _():
        if out_ref.shape[1] // (3 * LANES) > 1:
            for copy in copies(step - 1, 1 - slot):
                copy.wait()
        for copy in copies(step, slot):
            copy.wait()


def attend_backward(projected, segment_row, log_totals, grad_out):
    rows = projected.shape[0]
    width = projected.shape[1] // 3
    pairs = width // LANES
    block = min(256, rows)
    column = lambda part: pl.BlockSpec((rows, LANES), lambda i: (0, part * pairs + i))
    return pl.pallas_call(
        functools.partial(attend_backward_kernel, block=block),
        grid=(pairs,),
        in_specs=[
            column(0),
            column(1),
            column(2),
            pl.BlockSpec((rows, 1), lambda i: (0, 0)),
            pl.BlockSpec((1, rows), lambda i: (0, 0)),
            pl.BlockSpec((1, 8, rows), lambda i: (i, 0, 0)),
            pl.BlockSpec((rows, LANES), lambda i: (0, i)),
        ],
        out_specs=pl.BlockSpec(memory_space=pl.ANY),
        out_shape=jax.ShapeDtypeStruct((rows, 3 * width), BF16),
        scratch_shapes=[
            pltpu.VMEM((rows, rows), F32),
            pltpu.VMEM((rows, LANES), F32),
            pltpu.VMEM((rows, LANES), F32),
            pltpu.VMEM((2, 3, rows, LANES), BF16),
            pltpu.SemaphoreType.DMA((2, 3)),
        ],
        compiler_params=pltpu.CompilerParams(vmem_limit_bytes=VMEM_LIMIT),
        name="attend_backward",
    )(
        projected,
        projected,
        projected,
        segment_row.reshape(rows, 1),
        segment_row.reshape(1, rows),
        log_totals,
        grad_out,
    )


def assemble_kernel(place_ref, own_ref, *refs, keys, rows, half):
    count = len(keys)
    parts, out_ref = refs[: 2 * count], refs[2 * count]
    core = place_ref[0]
    mine = place_ref[1]
    out_ref[pl.ds(pl.multiple_of(mine * rows, 16), rows), :] = own_ref[...]
    for index, (other, first, size) in enumerate(keys):
        row = pl.multiple_of((mine ^ other) * rows + first, 16)
        for side in range(2):
            col = pl.multiple_of((core ^ side) * half, LANES)
            out_ref[pl.ds(row, size), pl.ds(col, half)] = parts[side * count + index][...]


def bit_list(count):
    bits, bit = [], 1
    while bit < count:
        bits.append(bit)
        bit *= 2
    return bits


def gather_weight(weight, place, split):
    rows, cols = weight.shape
    half = cols // 2
    shards_count = lax.axis_size("shard")
    mine = lax.dynamic_slice(weight, (0, place[0] * half), (rows, half))
    bits = bit_list(shards_count)
    size = rows // split
    keys, near = [], []
    for piece in range(split):
        order = bits if piece % 2 == 0 else bits[::-1]
        if split == 1:
            blocks = {0: mine}
        else:
            blocks = {0: mine[piece * size : (piece + 1) * size]}
        for bit in order:
            blocks.update({j ^ bit: swap(blocks[j], "shard", bit) for j in list(blocks)})
        for j in sorted(blocks):
            if j:
                keys.append((j, piece * size, size))
                near.append(blocks[j])
    far = [swap(block, "replica", 1) for block in near]
    count = len(keys)
    return pl.pallas_call(
        functools.partial(assemble_kernel, keys=tuple(keys), rows=rows, half=half),
        grid_spec=pltpu.PrefetchScalarGridSpec(
            num_scalar_prefetch=1,
            in_specs=[pl.BlockSpec(memory_space=pltpu.VMEM)] * (2 * count + 1),
            out_specs=pl.BlockSpec(memory_space=pltpu.VMEM),
        ),
        out_shape=jax.ShapeDtypeStruct((rows * shards_count, cols), weight.dtype),
        compiler_params=pltpu.CompilerParams(vmem_limit_bytes=VMEM_LIMIT),
        name="assemble",
    )(place, weight, *near, *far)


def gather_small(vectors, place):
    sizes = [v.shape[0] for v in vectors]
    packed = jnp.concatenate(vectors)
    packed = packed.reshape(1, packed.shape[0])
    shards_count = lax.axis_size("shard")
    blocks = [packed if j == 0 else swap(packed, "shard", j) for j in range(shards_count)]
    for bit in bit_list(shards_count):
        here = (place[1] & bit) != 0
        blocks = [jnp.where(here, blocks[j ^ bit], blocks[j]) for j in range(shards_count)]
    whole = jnp.concatenate(blocks, axis=0).astype(F32)
    out, first = [], 0
    for size in sizes:
        out.append(whole[:, first : first + size].reshape(shards_count * size))
        first += size
    return out


def halvings(rows, replicas):
    parts = 1
    while 2 * parts < replicas and rows % (32 * parts) == 0:
        parts *= 2
    return parts


def weight_gradient_kernel(place_ref, lhs_ref, rhs_ref, *refs, order, parts, size, add, steps):
    if add:
        recv_ref, keep_ref, send_ref, turned_ref, sorted_ref = refs
    else:
        send_ref, turned_ref, sorted_ref = refs
    mine, level = place_ref[1], place_ref[2]
    rows = parts * size

    @pl.when(pl.program_id(1) == 0)
    def _():
        turned_ref[...] = lhs_ref[...].T
        for index, other in enumerate(order if steps == 1 else (0,)):
            for part in range(parts):
                shard = (mine ^ other) if steps == 1 else 0
                first = pl.multiple_of(shard * rows + (level ^ part) * size, 16)
                sorted_ref[index * rows + part * size : index * rows + (part + 1) * size, :] = turned_ref[
                    pl.ds(first, size), :
                ]

    total = matmul(sorted_ref[...], rhs_ref[...])
    if not add:
        send_ref[...] = total.astype(BF16)
        return
    total = (total + recv_ref[...].astype(F32)).astype(BF16)
    if steps == 1:
        middle = total.shape[0] // 2
        keep_ref[...] = total[:middle]
        send_ref[...] = total[middle:]
    else:
        step = pl.program_id(0)

        @pl.when(step < steps // 2)
        def _():
            keep_ref[...] = total

        @pl.when(step >= steps // 2)
        def _():
            send_ref[...] = total


def weight_gradient(left, right, place, order, steps, chunk, received=None):
    tokens, rows_all = left.shape
    half = right.shape[1] // 2
    shards_count = len(order)
    rows = rows_all // shards_count
    parts = halvings(rows, lax.axis_size("replica"))
    size = rows // parts
    add = received is not None
    block = rows_all // steps
    chunks = half // chunk
    side = 0 if add else 1
    if steps == 1:
        left_spec = pl.BlockSpec((tokens, rows_all), lambda i, j, p: (0, 0))
    else:
        left_spec = pl.BlockSpec((tokens, block), lambda i, j, p: (0, p[1] ^ i))
    in_specs = [
        left_spec,
        pl.BlockSpec((tokens, chunk), lambda i, j, p: (0, (p[0] ^ side) * chunks + j)),
    ]
    whole = pl.BlockSpec((block, chunk), lambda i, j, p: (i, j))
    shape = lambda count: jax.ShapeDtypeStruct((count, half), BF16)
    if add:
        in_specs.append(whole)
        if steps == 1:
            part_spec = pl.BlockSpec((block // 2, chunk), lambda i, j, p: (0, j))
            out_specs = [part_spec, part_spec]
        else:
            middle = steps // 2
            out_specs = [
                pl.BlockSpec((block, chunk), lambda i, j, p: (jnp.minimum(i, middle - 1), j)),
                pl.BlockSpec((block, chunk), lambda i, j, p: (jnp.maximum(i - middle, 0), j)),
            ]
        out_shape = [shape(rows_all // 2), shape(rows_all // 2)]
    else:
        out_specs = whole
        out_shape = shape(rows_all)
    args = (left, right) + ((received,) if add else ())
    return pl.pallas_call(
        functools.partial(
            weight_gradient_kernel, order=tuple(order), parts=parts, size=size, add=add, steps=steps
        ),
        grid_spec=pltpu.PrefetchScalarGridSpec(
            num_scalar_prefetch=1,
            grid=(steps, chunks),
            in_specs=in_specs,
            out_specs=out_specs,
            scratch_shapes=[pltpu.VMEM((block, tokens), BF16), pltpu.VMEM((block, tokens), BF16)],
        ),
        out_shape=out_shape,
        compiler_params=pltpu.CompilerParams(vmem_limit_bytes=VMEM_LIMIT),
        name="weight_gradient",
    )(place, *args)


def add_low(left, right):
    return (left.astype(F32) + right.astype(F32)).astype(BF16)


def finish_kernel(place_ref, near_ref, far_ref, out_ref):
    out_ref[...] = jnp.where(pl.program_id(0) == 0, near_ref[...], far_ref[...]).astype(F32)


def reduce_rest(keep, send, place, bits, rows):
    half = keep.shape[1]
    replicas = lax.axis_size("replica")
    parts = halvings(rows, replicas)
    size = rows // parts
    for index, bit in enumerate(bits):
        total = add_low(keep, swap(send, "shard", bit))
        if index + 1 < len(bits):
            middle = total.shape[0] // 2
            keep, send = total[:middle], total[middle:]
    levels = bit_list(replicas)[1:]
    for bit in levels:
        if bit < 2 * parts:
            grid = total.reshape(total.shape[0] // (2 * size), 2, size, half)
            keep, send = grid[:, 0].reshape(-1, half), grid[:, 1].reshape(-1, half)
            total = add_low(keep, swap(send, "replica", bit))
        else:
            total = add_low(total, swap(total, "replica", bit))
    blocks = {0: total}
    for bit in reversed([b for b in levels if b < 2 * parts]):
        there = {j ^ (bit // 2): swap(blocks[j], "replica", bit) for j in list(blocks)}
        blocks.update(there)
    near = jnp.concatenate([blocks[j] for j in range(parts)], axis=0) if parts > 1 else total
    far = swap(near, "replica", 1)
    return pl.pallas_call(
        finish_kernel,
        grid_spec=pltpu.PrefetchScalarGridSpec(
            num_scalar_prefetch=1,
            grid=(2, parts),
            in_specs=[
                pl.BlockSpec((size, half), lambda i, j, p: (j, 0)),
                pl.BlockSpec((size, half), lambda i, j, p: (j, 0)),
            ],
            out_specs=pl.BlockSpec((size, half), lambda i, j, p: (p[2] % parts ^ j, p[0] ^ i)),
        ),
        out_shape=jax.ShapeDtypeStruct((rows, 2 * half), F32),
        name="finish",
    )(place, near, far)


def exchange_order(bits):
    order = [0]
    for bit in reversed(bits):
        order = order + [j ^ bit for j in order]
    return order


def reduce_small(parts, place):
    shards_count = lax.axis_size("shard")
    packed = jnp.concatenate([v.reshape(shards_count, -1) for v in parts], axis=1)
    for bit in bit_list(lax.axis_size("replica")):
        packed = packed + swap(packed, "replica", bit)
    for bit in bit_list(shards_count):
        packed = packed + swap(packed, "shard", bit)
    row = lax.dynamic_slice(packed, (place[1], 0), (1, packed.shape[1]))[0]
    out, first = [], 0
    for v in parts:
        size = v.shape[0] // shards_count
        out.append(row[first : first + size])
        first += size
    return out


def shards(
    tokens,
    segments,
    attention_gain,
    attention_shift,
    input_weight,
    query_bias,
    value_bias,
    mixing_weight,
    mixing_bias,
    dense_gain,
    dense_shift,
    expand_weight,
    expand_bias,
    contract_weight,
    contract_bias,
    cotangent,
):
    replica = lax.axis_index("replica")
    shard = lax.axis_index("shard")
    place = jnp.stack([replica & 1, shard, replica >> 1]).astype(jnp.int32)
    shards_count = lax.axis_size("shard")
    (
        gain_one,
        shift_one,
        query_full,
        value_full,
        mixing_bias_full,
        gain_two,
        shift_two,
        expand_bias_full,
        contract_bias_full,
    ) = gather_small(
        [
            attention_gain,
            attention_shift,
            query_bias,
            value_bias,
            mixing_bias,
            dense_gain,
            dense_shift,
            expand_bias,
            contract_bias,
        ],
        place,
    )
    input_full = gather_weight(input_weight, place, 2)
    mixing_full = gather_weight(mixing_weight, place, 1)
    expand_full = gather_weight(expand_weight, place, 2)
    contract_full = gather_weight(contract_weight, place, 2)
    seq_count, seq_rows, width = tokens.shape
    row_count = seq_count * seq_rows
    inputs = tokens.astype(F32).reshape(row_count, width)
    normed_one, norm_one_back = jax.vjp(layer_norm, inputs, gain_one, shift_one)
    normed_low = normed_one.astype(BF16)
    bias_all = jnp.concatenate([query_full, jnp.zeros_like(query_full), value_full])
    projected = (matmul(normed_low, input_full) + bias_all).astype(BF16)

    def rows_of(array, index):
        return array if seq_count == 1 else array[index * seq_rows : (index + 1) * seq_rows]

    def join(arrays):
        return arrays[0] if seq_count == 1 else jnp.concatenate(arrays, axis=0)

    forwards = [
        attend_forward(rows_of(projected, index), segments[index]) for index in range(seq_count)
    ]
    mixed_in = join([pair[0] for pair in forwards])
    middle = inputs + matmul(mixed_in, mixing_full) + mixing_bias_full
    normed_two, norm_two_back = jax.vjp(layer_norm, middle, gain_two, shift_two)
    normed_two_low = normed_two.astype(BF16)
    hidden_pre = matmul(normed_two_low, expand_full) + expand_bias_full
    hidden_full, gelu_back = jax.vjp(gelu_tanh, hidden_pre)
    hidden_act = hidden_full.astype(BF16)
    result = middle + matmul(hidden_act, contract_full) + contract_bias_full
    layer_output = result.astype(BF16).reshape(seq_count, seq_rows, width)

    bits = bit_list(shards_count)
    forth, back = bits, bits[::-1]
    order_forth, order_back = exchange_order(forth), exchange_order(back)
    identity = order_back == list(range(shards_count))
    grad_branch = cotangent.reshape(row_count, width)
    grad_result = grad_branch.astype(F32)
    contract_steps = shards_count if identity else 1
    contract_chunk = width // 2
    contract_sent = weight_gradient(
        hidden_act, grad_branch, place, order_back, contract_steps, contract_chunk
    )
    contract_got = swap(contract_sent, "replica", 1)
    grad_hidden = dot_cols(grad_branch, contract_full)
    grad_pre = gelu_back(grad_hidden)[0].astype(BF16)
    contract_pair = weight_gradient(
        hidden_act, grad_branch, place, order_back, contract_steps, contract_chunk, contract_got
    )
    contract_total = reduce_rest(*contract_pair, place, back, contract_weight.shape[0])
    expand_sent = weight_gradient(normed_two_low, grad_pre, place, order_forth, 1, 512)
    expand_got = swap(expand_sent, "replica", 1)
    grad_normed_two = dot_cols(grad_pre, expand_full)
    expand_pair = weight_gradient(
        normed_two_low, grad_pre, place, order_forth, 1, 512, expand_got
    )
    expand_total = reduce_rest(*expand_pair, place, forth, expand_weight.shape[0])
    contract_bias_grad = jnp.sum(grad_result, axis=0)
    expand_bias_grad = jnp.sum(grad_pre, axis=0, dtype=F32)
    grad_middle_norm, gain_two_grad, shift_two_grad = norm_two_back(grad_normed_two)
    grad_middle = grad_result + grad_middle_norm
    grad_mix = grad_middle.astype(BF16)
    mixing_bias_grad = jnp.sum(grad_mix, axis=0, dtype=F32)
    grad_attended = dot_cols(grad_mix, mixing_full).astype(BF16)
    mixing_sent = weight_gradient(mixed_in, grad_mix, place, order_back, 1, width // 2)
    mixing_got = swap(mixing_sent, "replica", 1)
    grad_projected = join(
        [
            attend_backward(
                rows_of(projected, index),
                segments[index],
                forwards[index][1],
                rows_of(grad_attended, index),
            )
            for index in range(seq_count)
        ]
    )
    mixing_pair = weight_gradient(
        mixed_in, grad_mix, place, order_back, 1, width // 2, mixing_got
    )
    mixing_total = reduce_rest(*mixing_pair, place, back, mixing_weight.shape[0])
    input_sent = weight_gradient(normed_low, grad_projected, place, order_forth, 1, width // 2)
    input_got = swap(input_sent, "replica", 1)
    projected_bias_grad = jnp.sum(grad_projected, axis=0, dtype=F32)
    query_grad = projected_bias_grad[:width]
    value_grad = projected_bias_grad[2 * width :]
    input_pair = weight_gradient(
        normed_low, grad_projected, place, order_forth, 1, width // 2, input_got
    )
    input_total = reduce_rest(*input_pair, place, forth, input_weight.shape[0])
    grad_normed_one = dot_cols(grad_projected, input_full)
    grad_inputs_norm, gain_one_grad, shift_one_grad = norm_one_back(grad_normed_one)
    tokens_gradient = (grad_middle + grad_inputs_norm).astype(BF16).reshape(seq_count, seq_rows, width)
    (
        attention_gain_total,
        attention_shift_total,
        query_total,
        value_total,
        mixing_bias_total,
        dense_gain_total,
        dense_shift_total,
        expand_bias_total,
        contract_bias_total,
    ) = reduce_small(
        [
            gain_one_grad,
            shift_one_grad,
            query_grad,
            value_grad,
            mixing_bias_grad,
            gain_two_grad,
            shift_two_grad,
            expand_bias_grad,
            contract_bias_grad,
        ],
        place,
    )
    return (
        layer_output,
        tokens_gradient,
        attention_gain_total,
        attention_shift_total,
        input_total,
        query_total,
        value_total,
        mixing_total,
        mixing_bias_total,
        dense_gain_total,
        dense_shift_total,
        expand_total,
        expand_bias_total,
        contract_total,
        contract_bias_total,
    )


def solution(mesh):
    return jax.shard_map(
        shards,
        mesh=mesh,
        in_specs=(
            P(("replica", "shard"), None, None),
            P(("replica", "shard"), None),
            P("shard"),
            P("shard"),
            P("shard", None),
            P("shard"),
            P("shard"),
            P("shard", None),
            P("shard"),
            P("shard"),
            P("shard"),
            P("shard", None),
            P("shard"),
            P("shard", None),
            P("shard"),
            P(("replica", "shard"), None, None),
        ),
        out_specs=(
            P(("replica", "shard"), None, None),
            P(("replica", "shard"), None, None),
            P("shard"),
            P("shard"),
            P("shard", None),
            P("shard"),
            P("shard"),
            P("shard", None),
            P("shard"),
            P("shard"),
            P("shard"),
            P("shard", None),
            P("shard"),
            P("shard", None),
            P("shard"),
        ),
        check_vma=False,
    )
```

```python
import functools

import jax
import jax.numpy as jnp
from jax import lax
from jax.experimental import pallas as pl
from jax.experimental.pallas import tpu as pltpu
from jax.sharding import PartitionSpec as P

H = 12
HD = 64
LANES = 128
EPSILON = 1e-05
NEG = -1e30
VMEM_LIMIT = 56 * 1024 * 1024


F32 = jnp.float32
BF16 = jnp.bfloat16


def layer_norm(value, gain, shift):
    center = jnp.mean(value, axis=-1, keepdims=True)
    centred = value - center
    spread = jnp.mean(centred * centred, axis=-1, keepdims=True)
    return centred * lax.rsqrt(spread + EPSILON) * gain + shift


def gelu_tanh(value):
    return jax.nn.gelu(value, approximate=True)


def matmul(left, right):
    return jnp.dot(left, right, preferred_element_type=F32)


def dot_cols(left, right):
    return lax.dot_general(left, right, (((1,), (1,)), ((), ())), preferred_element_type=F32)


def dot_rows(left, right):
    return lax.dot_general(left, right, (((0,), (0,)), ((), ())), preferred_element_type=F32)


def swap(value, axis, bit):
    count = lax.axis_size(axis)
    return lax.ppermute(value, axis, [(i, i ^ bit) for i in range(count)])


def attend_forward_kernel(q_ref, k_ref, v_ref, segc_ref, segr_ref, o_ref, lse_ref, bias_ref, *, block):
    rows = q_ref.shape[0]

    @pl.when(pl.program_id(0) == 0)
    def _():
        for first in range(0, rows, block):
            keys = first + block
            row_id = first + lax.broadcasted_iota(jnp.int32, (block, keys), 0)
            key_id = lax.broadcasted_iota(jnp.int32, (block, keys), 1)
            allowed = (segc_ref[first:keys, :] == segr_ref[:, :keys]) & (row_id >= key_id)
            bias_ref[first:keys, :keys] = jnp.where(allowed, 0.0, NEG)

    lane = lax.broadcasted_iota(jnp.int32, (1, LANES), 1)
    scale = jnp.asarray(HD ** (-0.5), BF16)
    for first in range(0, rows, block):
        keys = first + block
        query = q_ref[first:keys, :] * scale
        key_rows = k_ref[:keys, :]
        value_rows = v_ref[:keys, :]
        parts = []
        for head in range(LANES // HD):
            mine = lane // HD == head
            one = jnp.where(mine, query, jnp.zeros_like(query))
            score = dot_cols(one, key_rows) + bias_ref[first:keys, :keys]
            peak = jnp.max(score, axis=1, keepdims=True)
            expo = jnp.exp(score - peak)
            total = jnp.sum(expo, axis=1, keepdims=True)
            out = matmul(expo.astype(BF16), value_rows) / total
            parts.append(jnp.where(mine, out, 0.0))
            log_total = jnp.broadcast_to(peak + jnp.log(total), (block, LANES))
            lse_ref[0, head : head + 1, first:keys] = log_total.T[0:1, :]
        o_ref[first:keys, :] = sum(parts).astype(BF16)


def attend_forward(projected, segment_row):
    rows = projected.shape[0]
    width = projected.shape[1] // 3
    pairs = width // LANES
    block = min(256, rows)
    column = lambda part: pl.BlockSpec((rows, LANES), lambda i: (0, part * pairs + i))
    return pl.pallas_call(
        functools.partial(attend_forward_kernel, block=block),
        grid=(pairs,),
        in_specs=[
            column(0),
            column(1),
            column(2),
            pl.BlockSpec((rows, 1), lambda i: (0, 0)),
            pl.BlockSpec((1, rows), lambda i: (0, 0)),
        ],
        out_specs=[
            pl.BlockSpec((rows, LANES), lambda i: (0, i)),
            pl.BlockSpec((1, 8, rows), lambda i: (i, 0, 0)),
        ],
        out_shape=[
            jax.ShapeDtypeStruct((rows, width), BF16),
            jax.ShapeDtypeStruct((pairs, 8, rows), F32),
        ],
        scratch_shapes=[pltpu.VMEM((rows, rows), F32)],
        compiler_params=pltpu.CompilerParams(vmem_limit_bytes=VMEM_LIMIT),
        name="attend_forward",
    )(projected, projected, projected, segment_row.reshape(rows, 1), segment_row.reshape(1, rows))


def attend_backward_kernel(
    q_ref,
    k_ref,
    v_ref,
    segc_ref,
    segr_ref,
    lse_ref,
    do_ref,
    *refs,
    block,
    first_pair,
    pairs,
    steps_here,
):
    out_ref, bias_ref, dk_ref, dv_ref, stage_ref, sem = refs[-6:]
    rows = q_ref.shape[0]
    step = pl.program_id(0)
    steps = pl.num_programs(0)
    calls_steps = steps_here

    @pl.when(step == 0)
    def _():
        for first in range(0, rows, block):
            keys = first + block
            key_id = lax.broadcasted_iota(jnp.int32, (keys, block), 0)
            row_id = first + lax.broadcasted_iota(jnp.int32, (keys, block), 1)
            allowed = (segc_ref[:keys, :] == segr_ref[:, first:keys]) & (row_id >= key_id)
            bias_ref[:keys, first:keys] = jnp.where(allowed, 0.0, NEG)

    slot = step % 2

    def copies(at_step, at_slot):
        return [
            pltpu.make_async_copy(
                stage_ref.at[at_slot, part],
                out_ref.at[:, pl.ds(pl.multiple_of((part * pairs + first_pair + at_step) * LANES, LANES), LANES)],
                sem.at[at_slot, part],
            )
            for part in range(3)
        ]

    @pl.when(step >= 2)
    def _():
        for copy in copies(step - 2, slot):
            copy.wait()

    lane = lax.broadcasted_iota(jnp.int32, (1, LANES), 1)
    scale = jnp.asarray(HD ** (-0.5), BF16)
    for first in range(0, rows, block):
        keys = first + block
        query = q_ref[first:keys, :] * scale
        grad = do_ref[first:keys, :]
        key_rows = k_ref[:keys, :]
        value_rows = v_ref[:keys, :]
        shares, slopes, queries, grads, parts = [], [], [], [], []
        for head in range(LANES // HD):
            mine = lane // HD == head
            one = jnp.where(mine, query, jnp.zeros_like(query))
            one_grad = jnp.where(mine, grad, jnp.zeros_like(grad))
            score = dot_cols(key_rows, one) + bias_ref[:keys, first:keys]
            share = jnp.exp(score - lse_ref[0, head : head + 1, first:keys])
            grad_share = dot_cols(value_rows, one_grad)
            center = jnp.sum(share * grad_share, axis=0, keepdims=True)
            slope = (share * (grad_share - center)).astype(BF16)
            shares.append(share.astype(BF16))
            slopes.append(slope)
            queries.append(one)
            grads.append(one_grad)
            parts.append(jnp.where(mine, dot_rows(slope, key_rows), 0.0))
        value_part = sum(matmul(a, b) for a, b in zip(shares, grads))
        key_part = sum(matmul(a, b) for a, b in zip(slopes, queries))
        if first > 0:
            dv_ref[:first, :] += value_part[:first]
            dk_ref[:first, :] += key_part[:first]
        dv_ref[first:keys, :] = value_part[first:]
        dk_ref[first:keys, :] = key_part[first:]
        stage_ref[slot, 0, first:keys, :] = (sum(parts) * (HD ** (-0.5))).astype(BF16)
    stage_ref[slot, 1] = dk_ref[...].astype(BF16)
    stage_ref[slot, 2] = dv_ref[...].astype(BF16)
    for copy in copies(step, slot):
        copy.start()

    @pl.when(step == steps - 1)
    def _():
        if calls_steps > 1:
            for copy in copies(step - 1, 1 - slot):
                copy.wait()
        for copy in copies(step, slot):
            copy.wait()


def attend_backward(projected, segment_row, log_totals, grad_out, first_pair, count, before):
    rows = projected.shape[0]
    width = projected.shape[1] // 3
    pairs = width // LANES
    block = min(256, rows)
    column = lambda part: pl.BlockSpec((rows, LANES), lambda i: (0, part * pairs + first_pair + i))
    in_specs = [
        column(0),
        column(1),
        column(2),
        pl.BlockSpec((rows, 1), lambda i: (0, 0)),
        pl.BlockSpec((1, rows), lambda i: (0, 0)),
        pl.BlockSpec((1, 8, rows), lambda i: (first_pair + i, 0, 0)),
        pl.BlockSpec((rows, LANES), lambda i: (0, first_pair + i)),
    ]
    args = [
        projected,
        projected,
        projected,
        segment_row.reshape(rows, 1),
        segment_row.reshape(1, rows),
        log_totals,
        grad_out,
    ]
    aliases = {}
    if before is not None:
        in_specs.append(pl.BlockSpec(memory_space=pl.ANY))
        args.append(before)
        aliases = {7: 0}
    return pl.pallas_call(
        functools.partial(
            attend_backward_kernel, block=block, first_pair=first_pair, pairs=pairs, steps_here=count
        ),
        grid=(count,),
        in_specs=in_specs,
        out_specs=pl.BlockSpec(memory_space=pl.ANY),
        out_shape=jax.ShapeDtypeStruct((rows, 3 * width), BF16),
        scratch_shapes=[
            pltpu.VMEM((rows, rows), F32),
            pltpu.VMEM((rows, LANES), F32),
            pltpu.VMEM((rows, LANES), F32),
            pltpu.VMEM((2, 3, rows, LANES), BF16),
            pltpu.SemaphoreType.DMA((2, 3)),
        ],
        input_output_aliases=aliases,
        compiler_params=pltpu.CompilerParams(vmem_limit_bytes=VMEM_LIMIT),
        name="attend_backward",
    )(*args)


def assemble_kernel(place_ref, *refs, keys, rows, halves):
    count, kinds = len(keys), len(halves)
    owns, near, far, outs = refs[:kinds], refs[kinds : kinds + count], refs[kinds + count], refs[kinds + count + 1 :]
    core = place_ref[0]
    mine = place_ref[1]
    for own_ref, out_ref in zip(owns, outs):
        out_ref[pl.ds(pl.multiple_of(mine * rows, 16), rows), :] = own_ref[...]
    done = 0
    for index, (other, first, size) in enumerate(keys):
        row = pl.multiple_of((mine ^ other) * rows + first, 16)
        col = 0
        for half, out_ref in zip(halves, outs):
            left = pl.multiple_of(core * half, LANES)
            right = pl.multiple_of((1 - core) * half, LANES)
            out_ref[pl.ds(row, size), pl.ds(left, half)] = near[index][:, col : col + half]
            out_ref[pl.ds(row, size), pl.ds(right, half)] = far[done : done + size, col : col + half]
            col += half
        done += size


def bit_list(count):
    bits, bit = [], 1
    while bit < count:
        bits.append(bit)
        bit *= 2
    return bits


def column_half(weight, place):
    half = weight.shape[1] // 2
    return lax.dynamic_slice(weight, (0, place[0] * half), (weight.shape[0], half))


def gather_blocks(mine, orders):
    size = mine.shape[0] // len(orders)
    out = {}
    for piece, order in enumerate(orders):
        blocks = {0: mine[piece * size : (piece + 1) * size] if len(orders) > 1 else mine}
        for bit in order:
            blocks.update({j ^ bit: swap(blocks[j], "shard", bit) for j in list(blocks)})
        for j in sorted(blocks):
            if j:
                out[piece, j] = blocks[j]
    return out


def assemble(weights, blocks, place):
    rows = weights[0].shape[0]
    shards_count = lax.axis_size("shard")
    halves = tuple(w.shape[1] // 2 for w in weights)
    keys, near = [], []
    for (piece, other), block in blocks.items():
        keys.append((other, piece * block.shape[0], block.shape[0]))
        near.append(block)
    far = swap(jnp.concatenate(near, axis=0), "replica", 1)
    return pl.pallas_call(
        functools.partial(assemble_kernel, keys=tuple(keys), rows=rows, halves=halves),
        grid_spec=pltpu.PrefetchScalarGridSpec(
            num_scalar_prefetch=1,
            in_specs=[pl.BlockSpec(memory_space=pltpu.VMEM)] * (len(weights) + len(near) + 1),
            out_specs=[pl.BlockSpec(memory_space=pltpu.VMEM)] * len(weights),
        ),
        out_shape=[jax.ShapeDtypeStruct((rows * shards_count, w.shape[1]), w.dtype) for w in weights],
        compiler_params=pltpu.CompilerParams(vmem_limit_bytes=VMEM_LIMIT),
        name="assemble",
    )(place, *weights, *near, far)


def gather_small(vectors, place):
    sizes = [v.shape[0] for v in vectors]
    packed = jnp.concatenate(vectors)
    packed = packed.reshape(1, packed.shape[0])
    shards_count = lax.axis_size("shard")
    blocks = [packed if j == 0 else swap(packed, "shard", j) for j in range(shards_count)]
    for bit in bit_list(shards_count):
        here = (place[1] & bit) != 0
        blocks = [jnp.where(here, blocks[j ^ bit], blocks[j]) for j in range(shards_count)]
    whole = jnp.concatenate(blocks, axis=0).astype(F32)
    out, first = [], 0
    for size in sizes:
        out.append(whole[:, first : first + size].reshape(shards_count * size))
        first += size
    return out


def halvings(rows, replicas):
    parts = 1
    while 2 * parts < replicas and rows % (32 * parts) == 0:
        parts *= 2
    return parts


def weight_gradient_kernel(place_ref, lhs_ref, rhs_ref, *refs, order, got_order, parts, size, add, steps):
    if add:
        recv_ref, keep_ref, send_ref, turned_ref, sorted_ref = refs
    else:
        send_ref, turned_ref, sorted_ref = refs
    mine, level = place_ref[1], place_ref[2]
    rows = parts * size

    @pl.when(pl.program_id(1) == 0)
    def _():
        turned_ref[...] = lhs_ref[...].T
        for index, other in enumerate(order if steps == 1 else (0,)):
            for part in range(parts):
                shard = (mine ^ other) if steps == 1 else 0
                first = pl.multiple_of(shard * rows + (level ^ part) * size, 16)
                sorted_ref[index * rows + part * size : index * rows + (part + 1) * size, :] = turned_ref[
                    pl.ds(first, size), :
                ]

    total = matmul(sorted_ref[...], rhs_ref[...])
    if not add:
        send_ref[...] = total.astype(BF16)
        return
    if got_order == order:
        got = recv_ref[...]
    else:
        got = jnp.concatenate(
            [recv_ref[got_order.index(j) * rows : (got_order.index(j) + 1) * rows, :] for j in order], axis=0
        )
    total = (total + got.astype(F32)).astype(BF16)
    if steps == 1:
        middle = total.shape[0] // 2
        keep_ref[...] = total[:middle]
        send_ref[...] = total[middle:]
    else:
        step = pl.program_id(0)

        @pl.when(step < steps // 2)
        def _():
            keep_ref[...] = total

        @pl.when(step >= steps // 2)
        def _():
            send_ref[...] = total


def weight_gradient(left, right, place, order, steps, chunk, received=None, got_order=None, first=0, count=None):
    tokens, rows_all = left.shape
    half = right.shape[1] // 2
    shards_count = len(order)
    rows = rows_all // shards_count
    parts = halvings(rows, lax.axis_size("replica"))
    size = rows // parts
    add = received is not None
    block = rows_all // steps
    total_chunks = half // chunk
    chunks = total_chunks if count is None else count
    side = 0 if add else 1
    if steps == 1:
        left_spec = pl.BlockSpec((tokens, rows_all), lambda i, j, p: (0, 0))
    else:
        left_spec = pl.BlockSpec((tokens, block), lambda i, j, p: (0, p[1] ^ i))
    in_specs = [
        left_spec,
        pl.BlockSpec((tokens, chunk), lambda i, j, p: (0, (p[0] ^ side) * total_chunks + first + j)),
    ]
    whole = pl.BlockSpec((block, chunk), lambda i, j, p: (i, j))
    shape = lambda rows_out: jax.ShapeDtypeStruct((rows_out, chunks * chunk), BF16)
    if add:
        in_specs.append(pl.BlockSpec((block, chunk), lambda i, j, p: (i, first + j)))
        if steps == 1:
            part_spec = pl.BlockSpec((block // 2, chunk), lambda i, j, p: (0, j))
            out_specs = [part_spec, part_spec]
        else:
            middle = steps // 2
            out_specs = [
                pl.BlockSpec((block, chunk), lambda i, j, p: (jnp.minimum(i, middle - 1), j)),
                pl.BlockSpec((block, chunk), lambda i, j, p: (jnp.maximum(i - middle, 0), j)),
            ]
        out_shape = [shape(rows_all // 2), shape(rows_all // 2)]
    else:
        out_specs = whole
        out_shape = shape(rows_all)
    args = (left, right) + ((received,) if add else ())
    return pl.pallas_call(
        functools.partial(
            weight_gradient_kernel, order=tuple(order), got_order=tuple(got_order or order), parts=parts, size=size, add=add, steps=steps
        ),
        grid_spec=pltpu.PrefetchScalarGridSpec(
            num_scalar_prefetch=1,
            grid=(steps, chunks),
            in_specs=in_specs,
            out_specs=out_specs,
            scratch_shapes=[pltpu.VMEM((block, tokens), BF16), pltpu.VMEM((block, tokens), BF16)],
        ),
        out_shape=out_shape,
        compiler_params=pltpu.CompilerParams(vmem_limit_bytes=VMEM_LIMIT),
        name="weight_gradient",
    )(place, *args)


def add_low(left, right):
    return (left.astype(F32) + right.astype(F32)).astype(BF16)


def finish_kernel(place_ref, near_ref, far_ref, *outs, layout, parts):
    core = place_ref[0]
    level = place_ref[2] % parts
    size = near_ref.shape[0] // parts
    for part in range(parts):
        row = pl.multiple_of((level ^ part) * size, 8)
        for col, width, index, start in layout:
            out_ref = outs[index]
            half = out_ref.shape[1] // 2
            for side, ref in enumerate((near_ref, far_ref)):
                place = pl.multiple_of((core ^ side) * half + start, LANES)
                out_ref[pl.ds(row, size), pl.ds(place, width)] = ref[
                    part * size : (part + 1) * size, col : col + width
                ].astype(F32)


def reduce_shards(keep, send, bits):
    total = None
    for index, bit in enumerate(bits):
        total = add_low(keep, swap(send, "shard", bit))
        if index + 1 < len(bits):
            middle = total.shape[0] // 2
            keep, send = total[:middle], total[middle:]
    return total


def reduce_replicas(total, place, layout, shapes):
    rows, half = total.shape
    replicas = lax.axis_size("replica")
    parts = halvings(rows, replicas)
    size = rows // parts
    levels = bit_list(replicas)[1:]
    for bit in levels:
        if bit < 2 * parts:
            grid = total.reshape(total.shape[0] // (2 * size), 2, size, half)
            keep, send = grid[:, 0].reshape(-1, half), grid[:, 1].reshape(-1, half)
            total = add_low(keep, swap(send, "replica", bit))
        else:
            total = add_low(total, swap(total, "replica", bit))
    order = [0]
    for bit in reversed([b for b in levels if b < 2 * parts]):
        total = jnp.concatenate([total, swap(total, "replica", bit)], axis=0)
        order = order + [j ^ (bit // 2) for j in order]
    if order != list(range(parts)):
        total = jnp.concatenate([total[order.index(j) * size : (order.index(j) + 1) * size] for j in range(parts)])
    far = swap(total, "replica", 1)
    return pl.pallas_call(
        functools.partial(finish_kernel, layout=tuple(layout), parts=parts),
        grid_spec=pltpu.PrefetchScalarGridSpec(
            num_scalar_prefetch=1,
            in_specs=[pl.BlockSpec(memory_space=pltpu.VMEM)] * 2,
            out_specs=[pl.BlockSpec(memory_space=pltpu.VMEM)] * len(shapes),
        ),
        out_shape=[jax.ShapeDtypeStruct(shape, F32) for shape in shapes],
        compiler_params=pltpu.CompilerParams(vmem_limit_bytes=VMEM_LIMIT),
        name="finish",
    )(place, total, far)


def exchange_order(bits):
    order = [0]
    for bit in reversed(bits):
        order = order + [j ^ bit for j in order]
    return order


def reduce_small(parts, place):
    shards_count = lax.axis_size("shard")
    packed = jnp.concatenate([v.reshape(shards_count, -1) for v in parts], axis=1)
    for bit in bit_list(lax.axis_size("replica")):
        packed = packed + swap(packed, "replica", bit)
    for bit in bit_list(shards_count):
        packed = packed + swap(packed, "shard", bit)
    row = lax.dynamic_slice(packed, (place[1], 0), (1, packed.shape[1]))[0]
    out, first = [], 0
    for v in parts:
        size = v.shape[0] // shards_count
        out.append(row[first : first + size])
        first += size
    return out


def shards(
    tokens,
    segments,
    attention_gain,
    attention_shift,
    input_weight,
    query_bias,
    value_bias,
    mixing_weight,
    mixing_bias,
    dense_gain,
    dense_shift,
    expand_weight,
    expand_bias,
    contract_weight,
    contract_bias,
    cotangent,
):
    replica = lax.axis_index("replica")
    shard = lax.axis_index("shard")
    place = jnp.stack([replica & 1, shard, replica >> 1]).astype(jnp.int32)
    shards_count = lax.axis_size("shard")
    (
        gain_one,
        shift_one,
        query_full,
        value_full,
        mixing_bias_full,
        gain_two,
        shift_two,
        expand_bias_full,
        contract_bias_full,
    ) = gather_small(
        [
            attention_gain,
            attention_shift,
            query_bias,
            value_bias,
            mixing_bias,
            dense_gain,
            dense_shift,
            expand_bias,
            contract_bias,
        ],
        place,
    )
    bits = bit_list(shards_count)
    forth, back = bits, bits[::-1]
    input_blocks = gather_blocks(column_half(input_weight, place), [forth, back])
    after = [input_blocks[0, back[0]], input_blocks[1, forth[0]]]
    dense_half = jnp.concatenate([column_half(expand_weight, place), column_half(mixing_weight, place)], axis=1)
    dense_half, *after = lax.optimization_barrier((dense_half, *after))
    dense_blocks = gather_blocks(dense_half, [forth])
    contract_half = column_half(contract_weight, place)
    contract_half, after_dense = lax.optimization_barrier((contract_half, dense_blocks[0, forth[0]]))
    contract_blocks = gather_blocks(contract_half, [back])
    (input_full,) = assemble([input_weight], input_blocks, place)
    seq_count, seq_rows, width = tokens.shape
    row_count = seq_count * seq_rows
    inputs = tokens.astype(F32).reshape(row_count, width)
    normed_one, norm_one_back = jax.vjp(layer_norm, inputs, gain_one, shift_one)
    normed_low = normed_one.astype(BF16)
    bias_all = jnp.concatenate([query_full, jnp.zeros_like(query_full), value_full])
    projected = (matmul(normed_low, input_full) + bias_all).astype(BF16)

    def rows_of(array, index):
        return array if seq_count == 1 else array[index * seq_rows : (index + 1) * seq_rows]

    def join(arrays):
        return arrays[0] if seq_count == 1 else jnp.concatenate(arrays, axis=0)

    forwards = [
        attend_forward(rows_of(projected, index), segments[index]) for index in range(seq_count)
    ]
    mixed_in = join([pair[0] for pair in forwards])
    expand_full, mixing_full = assemble([expand_weight, mixing_weight], dense_blocks, place)
    middle = inputs + matmul(mixed_in, mixing_full) + mixing_bias_full
    normed_two, norm_two_back = jax.vjp(layer_norm, middle, gain_two, shift_two)
    normed_two_low = normed_two.astype(BF16)
    hidden_pre = matmul(normed_two_low, expand_full) + expand_bias_full
    hidden_full, gelu_back = jax.vjp(gelu_tanh, hidden_pre)
    hidden_act = hidden_full.astype(BF16)
    (contract_full,) = assemble([contract_weight], contract_blocks, place)

    order_forth, order_back = exchange_order(forth), exchange_order(back)
    identity = order_back == list(range(shards_count))
    grad_branch = cotangent.reshape(row_count, width)
    grad_result = grad_branch.astype(F32)
    contract_steps = shards_count if identity else 1
    contract_chunk = width // 2
    contract_sent = weight_gradient(
        hidden_act, grad_branch, place, order_back, contract_steps, contract_chunk
    )
    contract_got = swap(contract_sent, "replica", 1)
    grad_first, contract_sent = lax.optimization_barrier((grad_branch, contract_sent))
    grad_hidden = dot_cols(grad_first, contract_full)
    grad_pre = gelu_back(grad_hidden)[0].astype(BF16)
    expand_sent = weight_gradient(normed_two_low, grad_pre, place, order_forth, 1, 512)
    expand_got = swap(expand_sent, "replica", 1)
    grad_pre, expand_sent = lax.optimization_barrier((grad_pre, expand_sent))
    contract_pair = weight_gradient(
        hidden_act, grad_branch, place, order_back, contract_steps, contract_chunk, contract_got
    )
    grad_pre, *contract_pair = lax.optimization_barrier((grad_pre, *contract_pair))
    expand_pair = weight_gradient(
        normed_two_low, grad_pre, place, order_forth, 1, 512, expand_got
    )
    grad_pre, *expand_pair = lax.optimization_barrier((grad_pre, *expand_pair))
    grad_normed_two = dot_cols(grad_pre, expand_full)
    contract_bias_grad = jnp.sum(grad_result, axis=0)
    expand_bias_grad = jnp.sum(grad_pre, axis=0, dtype=F32)
    grad_middle_norm, gain_two_grad, shift_two_grad = norm_two_back(grad_normed_two)
    grad_middle = grad_result + grad_middle_norm
    grad_mix = grad_middle.astype(BF16)
    mixing_bias_grad = jnp.sum(grad_mix, axis=0, dtype=F32)
    mixing_sent = weight_gradient(mixed_in, grad_mix, place, order_back, 1, width // 2)
    mixing_got = swap(mixing_sent, "replica", 1)
    grad_mix, mixing_sent = lax.optimization_barrier((grad_mix, mixing_sent))
    grad_attended = dot_cols(grad_mix, mixing_full).astype(BF16)
    mixing_pair = weight_gradient(
        mixed_in, grad_mix, place, order_back, 1, width // 2, mixing_got
    )
    grad_attended, *mixing_pair = lax.optimization_barrier((grad_attended, *mixing_pair))
    pairs = width // LANES
    calls = 3 if pairs % 3 == 0 else 1
    grads = [None] * seq_count
    for call in range(calls):
        if call == calls - 1 and len(bits) > 1:
            contract_sum = add_low(contract_pair[0], swap(contract_pair[1], "shard", back[0]))
            expand_sum = add_low(expand_pair[0], swap(expand_pair[1], "shard", forth[0]))
            grad_attended, contract_sum, expand_sum = lax.optimization_barrier(
                (grad_attended, contract_sum, expand_sum)
            )
            middle_c, middle_e = contract_sum.shape[0] // 2, expand_sum.shape[0] // 2
            contract_total = reduce_shards(contract_sum[:middle_c], contract_sum[middle_c:], back[1:])
            expand_total = reduce_shards(expand_sum[:middle_e], expand_sum[middle_e:], forth[1:])
        grads = [
            attend_backward(
                rows_of(projected, index),
                segments[index],
                forwards[index][1],
                rows_of(grad_attended, index),
                call * (pairs // calls),
                pairs // calls,
                grads[index],
            )
            for index in range(seq_count)
        ]
    if len(bits) == 1:
        contract_total = reduce_shards(*contract_pair, back)
        expand_total = reduce_shards(*expand_pair, forth)
    grad_projected = join(grads)
    chunk = width // 2
    input_sent = weight_gradient(normed_low, grad_projected, place, order_forth, 1, chunk)
    input_got = swap(input_sent, "replica", 1)
    grad_projected, input_sent, contract_total, expand_total = lax.optimization_barrier(
        (grad_projected, input_sent, contract_total, expand_total)
    )
    (contract_total,) = reduce_replicas(
        contract_total, place, [(0, width // 2, 0, 0)], [contract_weight.shape]
    )
    (expand_total,) = reduce_replicas(
        expand_total, place, [(0, expand_weight.shape[1] // 2, 0, 0)], [expand_weight.shape]
    )
    projected_bias_grad = jnp.sum(grad_projected, axis=0, dtype=F32)
    query_grad = projected_bias_grad[:width]
    value_grad = projected_bias_grad[2 * width :]
    input_pair = weight_gradient(
        normed_low, grad_projected, place, order_forth, 1, chunk, input_got, order_forth, 0, 2
    )
    input_last = weight_gradient(
        normed_low, grad_projected, place, order_back, 1, chunk, input_got, order_forth, 2, 1
    )
    grad_projected, hidden_act, *input_pairs = lax.optimization_barrier(
        (grad_projected, hidden_act, *input_pair, *input_last)
    )
    narrow = jnp.concatenate(
        [
            reduce_shards(*mixing_pair, back),
            reduce_shards(*input_pairs[:2], forth),
            reduce_shards(*input_pairs[2:], back),
        ],
        axis=1,
    )
    mixing_total, input_total = reduce_replicas(
        narrow,
        place,
        [(0, chunk, 0, 0), (chunk, 2 * chunk, 1, 0), (3 * chunk, chunk, 1, 2 * chunk)],
        [mixing_weight.shape, input_weight.shape],
    )
    grad_normed_one = dot_cols(grad_projected, input_full)
    grad_inputs_norm, gain_one_grad, shift_one_grad = norm_one_back(grad_normed_one)
    tokens_gradient = (grad_middle + grad_inputs_norm).astype(BF16).reshape(seq_count, seq_rows, width)
    result = middle + matmul(hidden_act, contract_full) + contract_bias_full
    layer_output = result.astype(BF16).reshape(seq_count, seq_rows, width)
    (
        attention_gain_total,
        attention_shift_total,
        query_total,
        value_total,
        mixing_bias_total,
        dense_gain_total,
        dense_shift_total,
        expand_bias_total,
        contract_bias_total,
    ) = reduce_small(
        [
            gain_one_grad,
            shift_one_grad,
            query_grad,
            value_grad,
            mixing_bias_grad,
            gain_two_grad,
            shift_two_grad,
            expand_bias_grad,
            contract_bias_grad,
        ],
        place,
    )
    return (
        layer_output,
        tokens_gradient,
        attention_gain_total,
        attention_shift_total,
        input_total,
        query_total,
        value_total,
        mixing_total,
        mixing_bias_total,
        dense_gain_total,
        dense_shift_total,
        expand_total,
        expand_bias_total,
        contract_total,
        contract_bias_total,
    )


def solution(mesh):
    return jax.shard_map(
        shards,
        mesh=mesh,
        in_specs=(
            P(("replica", "shard"), None, None),
            P(("replica", "shard"), None),
            P("shard"),
            P("shard"),
            P("shard", None),
            P("shard"),
            P("shard"),
            P("shard", None),
            P("shard"),
            P("shard"),
            P("shard"),
            P("shard", None),
            P("shard"),
            P("shard", None),
            P("shard"),
            P(("replica", "shard"), None, None),
        ),
        out_specs=(
            P(("replica", "shard"), None, None),
            P(("replica", "shard"), None, None),
            P("shard"),
            P("shard"),
            P("shard", None),
            P("shard"),
            P("shard"),
            P("shard", None),
            P("shard"),
            P("shard"),
            P("shard"),
            P("shard", None),
            P("shard"),
            P("shard", None),
            P("shard"),
        ),
        check_vma=False,
    )
```
